256 devices in a mesh: ctx: 32 (over y, x, core), head: 8 (over z).
Axes of the slice: x: 4, y: 4, z: 8, core: 2. Of those that a mesh axis runs over, the one named last changes fastest.
Arguments:
- queries: bfloat16 [8192, 16384], P(('ctx', 'head')), may hold values from -6 to 6
- keys: bfloat16 [8192, 1024], P(('ctx', 'head')), may hold values from -8 to 8
- values: bfloat16 [8192, 1024], P(('ctx', 'head')), may hold values from -4 to 4
- doc_ids: int32 [8192], replicated, may hold values from 0 to 15, never falling along the last dimension, each value on 1 to 769 neighbouring positions
- grad_out: bfloat16 [8192, 16384], P(('ctx', 'head')), may hold values from -4 to 4
Outputs:
- attn_out: bfloat16 [8192, 16384], P(('ctx', 'head'))
- grad_queries: bfloat16 [8192, 16384], P(('ctx', 'head'))
- grad_keys: bfloat16 [8192, 1024], P(('ctx', 'head'))
- grad_values: bfloat16 [8192, 1024], P(('ctx', 'head'))
The draws below stay inside these ranges and needn't reach their ends.
Inputs may be any that keep to these rules, and one draw needn't show every extreme that they name: `doc_ids`: document numbers never fall along the sequence; every document holds 1 to 769 tokens and one holds exactly 769.
All inputs are finite; a program needn't handle non-finite values.
Results may differ from the reference program's by a relative error of at most 0.025.
Values may be sent and summed in bfloat16 or wider, within the bound.
A program may use at most 64 MiB of HBM per device.

```python
import math
import jax
import jax.numpy as jnp
import numpy as np
from jax import lax

QHEADS = 128
KV_GROUPS = 8
HEAD_DIM = 128
TOK_DEV = 256
SPAN = 3
TOKENS = 8192
DOC_MOST = 769
DOC_COUNT = 16


def draw_queries(key, part):
    values_draw = jnp.clip(jax.random.normal(jax.random.fold_in(key, 1), (TOKENS, QHEADS * HEAD_DIM), jnp.float32), -4.0, 4.0)
    return values_draw.astype(jnp.bfloat16)


def draw_keys(key, part):
    values_draw = jnp.clip(jax.random.normal(jax.random.fold_in(key, 3), (TOKENS, KV_GROUPS * HEAD_DIM), jnp.float32), -4.0, 4.0)
    return values_draw.astype(jnp.bfloat16)


def shard_levels(rng, shape, cuts, smallest, largest):
    factor_of = 1.0
    for position, shards_of in cuts:
        steps = jax.random.uniform(jax.random.fold_in(jax.random.fold_in(rng, 6), position), (shards_of,), jnp.float32, smallest / len(cuts), largest / len(cuts))
        factor_of = factor_of * jnp.repeat(jnp.exp(steps), shape[position] // shards_of).reshape((-1,) + (1,) * (len(shape) - 1 - position))
    return factor_of


def length_profile(amount, total, bound, skew):
    portions = [(1 << 20) // math.isqrt(standing ** skew) + 1 for standing in range(2, amount + 1)]
    surplus, holding = total - bound - (amount - 1), [1] * (amount - 1)
    while surplus > 0:
        movable = [i for i in range(amount - 1) if holding[i] < bound]
        whole, remaining = sum([portions[i] for i in movable]), surplus
        for i in movable:
            extra = min(bound - holding[i], max(1, remaining * portions[i] // whole), surplus)
            holding[i] = holding[i] + extra
            surplus = surplus - extra
    return np.array([bound] + holding)


def ragged(stream_key, amount, total, limit, lean):
    if amount == 2:
        one = jax.random.randint(stream_key, (), max(1, total - limit), min(limit, total - 1) + 1)
        return jnp.stack([one, total - one])
    tallies = jnp.asarray(length_profile(amount, total, limit, lean), jnp.int32)
    twos = (amount - 1) // 2
    donor, taker = tallies[1:1 + 2 * twos:2], tallies[2:2 + 2 * twos:2]
    slack = jnp.minimum(donor - 1, limit - taker)
    shifted = jax.random.randint(jax.random.fold_in(stream_key, 1), (twos,), 0, 1 << 20) % (slack + 1)
    tallies = tallies.at[1:1 + 2 * twos:2].set(donor - shifted).at[2:2 + 2 * twos:2].set(taker + shifted)
    return tallies[jax.random.permutation(jax.random.fold_in(stream_key, 2), amount)]


def bell_draw(rng, dims, spread, reach, shards=(), kind=jnp.bfloat16):
    drawn = spread * jax.random.normal(rng, dims, jnp.float32)
    if shards:
        drawn = drawn * shard_levels(rng, dims, shards, -0.22, 0.18)
    return jnp.clip(drawn, -reach, reach).astype(kind)


def setup_inputs(seed: int = 0) -> dict:
    key_list = jax.random.split(jax.random.key(seed), 6)
    return {
        "queries": draw_queries(jax.random.fold_in(key_list[5], 71), 0),
        "keys": draw_keys(jax.random.fold_in(key_list[5], 71), 0),
        "values": bell_draw(key_list[2], (TOKENS, KV_GROUPS * HEAD_DIM), 1.0, 4.0, ((0, 256),)),
        "doc_ids": jnp.searchsorted(jnp.cumsum(ragged(key_list[3], DOC_COUNT, TOKENS, DOC_MOST, 2)), jnp.arange(TOKENS), side="right").astype(jnp.int32),
        "grad_out": bell_draw(key_list[4], (TOKENS, QHEADS * HEAD_DIM), 1.0, 4.0, ((0, 256),)),
    }


masked_fill = -1e+30

def reference(queries, keys, values, doc_ids, grad_out):
    row_count = TOK_DEV
    blocks = TOKENS // TOK_DEV
    window = SPAN + 1
    groups = KV_GROUPS
    group_size = QHEADS // KV_GROUPS
    head_width = HEAD_DIM
    score_scale = 1.0 / math.sqrt(head_width)
    pad_rows = SPAN * row_count
    key_pad = jnp.concatenate([jnp.zeros((pad_rows, groups * head_width), keys.dtype), keys], 0)
    key_pad = key_pad.reshape(blocks + SPAN, row_count, groups, head_width)
    val_pad = jnp.concatenate([jnp.zeros((pad_rows, groups * head_width), values.dtype), values], 0)
    val_pad = val_pad.reshape(blocks + SPAN, row_count, groups, head_width)
    doc_pad = jnp.concatenate([jnp.full((pad_rows,), -1, jnp.int32), doc_ids.astype(jnp.int32)], 0)
    doc_pad = doc_pad.reshape(blocks + SPAN, row_count)
    query_blocks = queries.reshape(blocks, row_count, groups, group_size, head_width)
    dout_blocks = grad_out.reshape(blocks, row_count, groups, group_size, head_width)
    doc_blocks = doc_ids.astype(jnp.int32).reshape(blocks, row_count)
    offsets = jnp.arange(row_count, dtype=jnp.int32)
    lags = jnp.arange(window, dtype=jnp.int32)

    def one_block(carry, block):
        grad_k, grad_v = carry
        query_blk = lax.dynamic_index_in_dim(query_blocks, block, 0, keepdims=False).astype(jnp.float32)
        dout_blk = lax.dynamic_index_in_dim(dout_blocks, block, 0, keepdims=False).astype(jnp.float32)
        key_win = lax.dynamic_slice_in_dim(key_pad, block, window, 0).astype(jnp.float32)
        val_win = lax.dynamic_slice_in_dim(val_pad, block, window, 0).astype(jnp.float32)
        doc_win = lax.dynamic_slice_in_dim(doc_pad, block, window, 0)
        query_doc = lax.dynamic_index_in_dim(doc_blocks, block, 0, keepdims=False)
        query_pos = block * row_count + offsets
        key_pos = (block - SPAN + lags)[:, None] * row_count + offsets[None, :]
        allowed = (query_doc[:, None, None] == doc_win[None]) & (key_pos[None] <= query_pos[:, None, None])
        mask = allowed[None, None]
        scores = jnp.einsum('igrd,wjgd->griwj', query_blk, key_win) * score_scale
        masked = jnp.where(mask, scores, masked_fill)
        blk_max = lax.optimization_barrier(jnp.max(masked, axis=-1))
        exp_terms = jnp.where(mask, jnp.exp(masked - blk_max[..., None]), 0.0)
        blk_sum = lax.optimization_barrier(jnp.sum(exp_terms, axis=-1))
        blk_weight = lax.optimization_barrier(exp_terms.astype(jnp.bfloat16)).astype(jnp.float32)
        blk_out = jnp.einsum('griwj,wjgd->griwd', blk_weight, val_win)
        run_max = lax.optimization_barrier(jnp.max(blk_max, axis=-1))
        factor = jnp.exp(blk_max - run_max[..., None])
        run_sum = lax.optimization_barrier(jnp.sum(factor * blk_sum, axis=-1))
        log_norm = run_max + jnp.log(run_sum)
        attn_heads = (lax.optimization_barrier(jnp.sum(factor[..., None] * blk_out, axis=-2)) / run_sum[..., None]).astype(jnp.bfloat16)
        row_delta = lax.optimization_barrier(jnp.sum(dout_blk.transpose(1, 2, 0, 3) * attn_heads.astype(jnp.float32), axis=-1))
        attn_prob = jnp.where(mask, jnp.exp(masked - log_norm[..., None, None]), 0.0)
        prob_round = lax.optimization_barrier(attn_prob.astype(jnp.bfloat16)).astype(jnp.float32)
        dv_window = jnp.einsum('griwj,igrd->wjgd', prob_round, dout_blk)
        grad_prob = jnp.einsum('igrd,wjgd->griwj', dout_blk, val_win)
        grad_score = attn_prob * (grad_prob - row_delta[..., None, None]) * score_scale
        grad_score = lax.optimization_barrier(grad_score.astype(jnp.bfloat16)).astype(jnp.float32)
        grad_query = jnp.einsum('griwj,wjgd->igrd', grad_score, key_win).astype(jnp.bfloat16)
        dk_window = jnp.einsum('griwj,igrd->wjgd', grad_score, query_blk)
        grad_k = lax.dynamic_update_slice_in_dim(grad_k, lax.dynamic_slice_in_dim(grad_k, block, window, 0) + dk_window, block, 0)
        grad_v = lax.dynamic_update_slice_in_dim(grad_v, lax.dynamic_slice_in_dim(grad_v, block, window, 0) + dv_window, block, 0)
        return ((grad_k, grad_v), (attn_heads.transpose(2, 0, 1, 3), grad_query))
    zeros_kv = jnp.zeros((blocks + SPAN, row_count, groups, head_width), jnp.float32)
    (grad_k, grad_v), (attn_all, grad_q_all) = lax.scan(one_block, (zeros_kv, zeros_kv), jnp.arange(blocks, dtype=jnp.int32))
    attn_out = attn_all.reshape(TOKENS, QHEADS * head_width)
    grad_queries = grad_q_all.reshape(TOKENS, QHEADS * head_width)
    grad_keys = grad_k[SPAN:].reshape(TOKENS, groups * head_width).astype(jnp.bfloat16)
    grad_values = grad_v[SPAN:].reshape(TOKENS, groups * head_width).astype(jnp.bfloat16)
    return (attn_out, grad_queries, grad_keys, grad_values)
```

```python
import functools
import math

import jax
import jax.numpy as jnp
from jax import lax
from jax.experimental import pallas as pl
from jax.experimental.pallas import tpu as pltpu
from jax.sharding import PartitionSpec as P

HEAD = 128
ROWS = 32
SLOTS = 5
WIN = 800
GROUP_HEADS = 16
SCALE = 1.0 / math.sqrt(HEAD)
LOG2E = math.log2(math.e)
NEG = -1e30


def attend(z, s, qs, dos, k_win, v_win, start):
    f32, bf16 = jnp.float32, jnp.bfloat16
    q_t = qs.T
    do_t = dos.T.astype(f32)
    kk = lax.broadcasted_iota(jnp.int32, (WIN, 128), 0)
    tt = lax.broadcasted_iota(jnp.int32, (WIN, 128), 1) % ROWS
    allowed = (kk >= start) & (kk <= tt + (WIN - ROWS))
    bias = jnp.where(allowed, 0.0, NEG).astype(f32)
    bias = jnp.concatenate([bias] * (GROUP_HEADS * ROWS // 128), axis=1)
    x = jnp.dot(k_win, q_t, preferred_element_type=f32) * (SCALE * LOG2E) + bias
    top = jnp.max(x, axis=0, keepdims=True)
    p = jnp.exp2(x - top)
    total = jnp.sum(p, axis=0, keepdims=True)
    pb = p.astype(bf16)
    inv = 1.0 / total
    out_t = (jnp.dot(v_win.T, pb, preferred_element_type=f32) * inv).astype(bf16)
    delta = jnp.sum(do_t * out_t.astype(f32), axis=0, keepdims=True) * inv
    do_n = (do_t * inv).astype(bf16)
    gp = jnp.dot(v_win, do_n, preferred_element_type=f32)
    gs = (pb.astype(f32) * (gp - delta)).astype(bf16)
    nt = (((1,), (1,)), ((), ()))
    gv = lax.dot_general(pb, do_n, nt, preferred_element_type=f32)
    gk = jnp.dot(gs, qs, preferred_element_type=f32) * SCALE
    gq_t = (jnp.dot(k_win.T, gs, preferred_element_type=f32) * SCALE).astype(bf16)
    return out_t.T, gq_t.T, gk, gv


def stack_heads(x):
    return jnp.concatenate([x[:, h * HEAD:(h + 1) * HEAD] for h in range(GROUP_HEADS)], axis=0)


def spread_heads(ref, x):
    for h in range(GROUP_HEADS):
        ref[0, :, h * HEAD:(h + 1) * HEAD] = x[h * ROWS:(h + 1) * ROWS, :]


def kernel(start_ref, q_ref, do_ref, k_ref, v_ref, o_ref, gq_ref, gk_ref, gv_ref, gk_acc, gv_acc):
    z = lax.axis_index("head")
    s = pl.program_id(1)
    off = pl.multiple_of(s * 256 + z * ROWS, ROWS)
    window = pl.ds(off, WIN)

    @pl.when(s == 0)
    def _():
        gk_acc[...] = jnp.zeros_like(gk_acc)
        gv_acc[...] = jnp.zeros_like(gv_acc)

    out, gq, gk, gv = attend(
        z, s, stack_heads(q_ref[0]), stack_heads(do_ref[0]), k_ref[window, :], v_ref[window, :], start_ref[0]
    )
    spread_heads(o_ref, out)
    spread_heads(gq_ref, gq)
    gk_acc[window, :] += gk
    gv_acc[window, :] += gv

    @pl.when(s == 1)
    def _():
        gk_ref[...] = gk_acc[...].astype(gk_ref.dtype)
        gv_ref[...] = gv_acc[...].astype(gv_ref.dtype)


def compute(starts, q2, do2, k_all, v_all):
    groups = k_all.shape[1] // HEAD
    width = GROUP_HEADS * HEAD
    rows = SLOTS * 256
    tok = pl.BlockSpec((1, ROWS, width), lambda g, s: (s, 0, g))
    key = pl.BlockSpec((rows, HEAD), lambda g, s: (0, g))
    bf16 = jnp.bfloat16
    return pl.pallas_call(
        kernel,
        grid=(groups, 2),
        out_shape=(
            jax.ShapeDtypeStruct(q2.shape, bf16),
            jax.ShapeDtypeStruct(q2.shape, bf16),
            jax.ShapeDtypeStruct(k_all.shape, bf16),
            jax.ShapeDtypeStruct(k_all.shape, bf16),
        ),
        in_specs=[pl.BlockSpec((1, 1, 128), lambda g, s: (s, 0, 0)), tok, tok, key, key],
        out_specs=(tok, tok, key, key),
        scratch_shapes=[pltpu.VMEM((rows, HEAD), jnp.float32)] * 2,
    )(starts, q2, do2, k_all, v_all)


def window_starts(doc_ids, first):
    ids = lax.dynamic_slice_in_dim(doc_ids, first, ROWS)
    begin = jnp.sum((doc_ids[None, :] < ids[:, None]).astype(jnp.int32), axis=1)
    rel = begin - (first - (WIN - ROWS))
    return jnp.tile(rel, 128 // ROWS)[None, :]


def local(queries, keys, values, doc_ids, grad_out):
    c = lax.axis_index("ctx")
    z = lax.axis_index("head")
    n = lax.axis_size("ctx")
    g = c % 2
    pair = c // 2
    swap = [(j, j ^ 1) for j in range(n)]
    ahead = [(j, (j + 2) % n) for j in range(n)]
    back = [(j, (j - 2) % n) for j in range(n)]

    def halves(x):
        half = x.shape[1] // 2
        mine = lax.dynamic_slice_in_dim(x, g * half, half, 1)
        other = lax.dynamic_slice_in_dim(x, (1 - g) * half, half, 1)
        got = lax.ppermute(other, "ctx", swap)
        return jnp.where(g == 0, jnp.stack([mine, got]), jnp.stack([got, mine]))

    def unhalve(x):
        mine = lax.dynamic_index_in_dim(x, g, 0, keepdims=False)
        other = lax.dynamic_index_in_dim(x, 1 - g, 0, keepdims=False)
        got = lax.ppermute(other, "ctx", swap)
        low = jnp.where(g == 0, mine, got)
        high = jnp.where(g == 0, got, mine)
        return jnp.concatenate([low, high], axis=1)

    def gather(x):
        own = halves(x)
        near = lax.ppermute(own, "ctx", ahead)
        far = lax.ppermute(near[1:], "ctx", ahead)
        five = jnp.concatenate([far, near, own], axis=0)
        return lax.all_gather(five, "head", axis=1, tiled=True).reshape(SLOTS * 256, -1)

    def scatter(x):
        five = lax.psum_scatter(x.reshape(SLOTS, 256, -1), "head", scatter_dimension=1, tiled=True).astype(jnp.float32)
        far = lax.ppermute(five[:1], "ctx", back)
        near = jnp.concatenate([five[1:2], five[2:3] + far], axis=0)
        near = lax.ppermute(near, "ctx", back)
        return unhalve(five[3:5] + near).astype(jnp.bfloat16)

    first = pair * 512 + z * ROWS
    starts = jnp.stack([window_starts(doc_ids, first), window_starts(doc_ids, first + 256)])
    q2, do2 = halves(queries), halves(grad_out)
    k_all, v_all = gather(keys), gather(values)
    o2, gq2, gk, gv = compute(starts, q2, do2, k_all, v_all)
    return unhalve(o2), unhalve(gq2), scatter(gk), scatter(gv)


def solution(mesh):
    spec = P(("ctx", "head"), None)
    return jax.shard_map(
        local,
        mesh=mesh,
        in_specs=(spec, spec, spec, P(), spec),
        out_specs=(spec, spec, spec, spec),
        check_vma=False,
    )
```

```python
import math

import jax
import jax.numpy as jnp
from jax import lax
from jax.experimental import pallas as pl
from jax.experimental.pallas import tpu as pltpu
from jax.sharding import PartitionSpec as P

HEAD = 128
ROWS = 32
SLOTS = 5
WIN = 800
GROUP_HEADS = 16
GROUPS = 4
KV = 2 * HEAD
RING = 8
HOPS = 4
SCALE = 1.0 / math.sqrt(HEAD)
LOG2E = math.log2(math.e)
NEG = -1e30
MESH = pl.DeviceIdType.MESH
STREAMS = ((3, 4), (1, 2), (0,))


def attend(qs, dos, k_win, v_win, start):
    f32, bf16 = jnp.float32, jnp.bfloat16
    q_t = qs.T
    do_t = dos.T.astype(f32)
    kk = lax.broadcasted_iota(jnp.int32, (WIN, 128), 0)
    tt = lax.broadcasted_iota(jnp.int32, (WIN, 128), 1) % ROWS
    allowed = (kk >= start) & (kk <= tt + (WIN - ROWS))
    bias = jnp.where(allowed, 0.0, NEG).astype(f32)
    bias = jnp.concatenate([bias] * (GROUP_HEADS * ROWS // 128), axis=1)
    x = jnp.dot(k_win, q_t, preferred_element_type=f32) * (SCALE * LOG2E) + bias
    top = jnp.max(x, axis=0, keepdims=True)
    p = jnp.exp2(x - top)
    total = jnp.sum(p, axis=0, keepdims=True)
    pb = p.astype(bf16)
    inv = 1.0 / total
    out_t = (jnp.dot(v_win.T, pb, preferred_element_type=f32) * inv).astype(bf16)
    delta = jnp.sum(do_t * out_t.astype(f32), axis=0, keepdims=True) * inv
    do_n = (do_t * inv).astype(bf16)
    gp = jnp.dot(v_win, do_n, preferred_element_type=f32)
    gs = (pb.astype(f32) * (gp - delta)).astype(bf16)
    nt = (((1,), (1,)), ((), ()))
    gv = lax.dot_general(pb, do_n, nt, preferred_element_type=f32)
    gk = jnp.dot(gs, qs, preferred_element_type=f32) * SCALE
    gq_t = (jnp.dot(k_win.T, gs, preferred_element_type=f32) * SCALE).astype(bf16)
    return out_t.T, gq_t.T, gk, gv


def stack_heads(x):
    return jnp.concatenate([x[:, h * HEAD:(h + 1) * HEAD] for h in range(GROUP_HEADS)], axis=0)


def kernel(
    start_ref, q_hbm, do_hbm, k_hbm, v_hbm,
    o_hbm, gq_hbm, gk_hbm, gv_hbm,
    kv, qd, og, acc, ring_out, ring_in, x_out, x_in, fin,
    kv_loc, kv_send, kv_recv, qd_loc, qd_send, qd_recv,
    gx_send, gx_recv, gz_send, gz_recv,
    rz_send, rz_recv, rx_send, rx_recv,
    o_loc, o_send, o_recv, f_loc, f_send, f_recv,
):
    f32, bf16 = jnp.float32, jnp.bfloat16
    c = lax.axis_index("ctx")
    z = lax.axis_index("head")
    n = lax.axis_size("ctx")
    g = lax.rem(c, 2)
    other = 1 - g
    partner = {"ctx": c + 1 - 2 * g, "head": z}
    ahead = {"ctx": lax.rem(c + 2, n), "head": z}
    behind = {"ctx": lax.rem(c + n - 2, n), "head": z}
    right = {"ctx": c, "head": lax.rem(z + 1, RING)}
    left = {"ctx": c, "head": lax.rem(z + RING - 1, RING)}
    sides = (right, left)
    half = GROUPS * HEAD
    wide = GROUPS * GROUP_HEADS * HEAD

    barrier = pltpu.get_barrier_semaphore()
    for peer in (partner, ahead, behind, right, left):
        pl.semaphore_signal(barrier, inc=1, device_id=peer, device_id_type=MESH)
    pl.semaphore_wait(barrier, 5)

    def remote(src, dst, send, recv, device):
        return pltpu.make_async_remote_copy(
            src_ref=src, dst_ref=dst, send_sem=send, recv_sem=recv, device_id=device, device_id_type=MESH
        )

    def rows(slot, block):
        return pl.ds(pl.multiple_of(slot * (RING * ROWS) + block * ROWS, ROWS), ROWS)

    def cols(group, which):
        return pl.ds(pl.multiple_of(which * half + group * HEAD, HEAD), HEAD)

    drains = []

    local_kv, remote_kv = [], []
    for t, src in enumerate((k_hbm, v_hbm)):
        for j in range(GROUPS):
            dst = kv.at[j, rows(3 + g, z), pl.ds(t * HEAD, HEAD)]
            remote_kv.append(remote(src.at[:, cols(j, other)], dst, kv_send.at[t, j], kv_recv.at[t, j], partner))
            local_kv.append(pltpu.make_async_copy(src.at[:, cols(j, g)], dst, kv_loc.at[t, j]))
    for copy in remote_kv + local_kv:
        copy.start()
    local_qd, remote_qd = [], []
    for t, src in enumerate((q_hbm, do_hbm)):
        mine = src.at[:, pl.ds(pl.multiple_of(g * wide, wide), wide)]
        theirs = src.at[:, pl.ds(pl.multiple_of(other * wide, wide), wide)]
        remote_qd.append(remote(theirs, qd.at[t, g], qd_send.at[t], qd_recv.at[t], partner))
        local_qd.append(pltpu.make_async_copy(mine, qd.at[t, g], qd_loc.at[t]))

    for copy in local_kv:
        copy.wait()
    for t, src in enumerate((k_hbm, v_hbm)):
        for j in range(GROUPS):
            dst = kv.at[j, rows(3 + other, z), pl.ds(t * HEAD, HEAD)]
            remote(src.at[:, cols(j, g)], dst, kv_send.at[t, j], kv_recv.at[t, j], partner).wait_recv()
    drains += remote_kv

    def block_of(direction, distance):
        if direction == 0:
            return lax.rem(z + RING - distance, RING)
        return lax.rem(z + distance, RING)

    def lanes(direction, hop):
        if hop < HOPS:
            return pl.ds(0, KV)
        return pl.ds(direction * HEAD, HEAD)

    def gather_copy(slot, direction, hop, distance):
        block = kv.at[:, rows(slot, block_of(direction, distance)), lanes(direction, hop)]
        return remote(
            block, block, gz_send.at[slot, direction, hop - 1], gz_recv.at[slot, direction, hop - 1], sides[direction]
        )

    def shift_copy(index, source, target):
        return remote(
            kv.at[:, rows(source, z), :], kv.at[:, rows(target, z), :], gx_send.at[index], gx_recv.at[index], ahead
        )

    shifts = [shift_copy(0, 3, 1), shift_copy(1, 4, 2), shift_copy(2, 2, 0)]
    shift_in = {1: shifts[0], 2: shifts[1], 0: shifts[2]}

    for step in range(1, HOPS + 4):
        for first, stream in enumerate(STREAMS):
            hop = step - first
            if hop < 1 or hop > HOPS + 1:
                continue
            for slot in stream:
                if hop == 1:
                    if slot < 3:
                        shift_in[slot].wait_recv()
                    if slot == 2:
                        shifts[2].start()
                        drains.append(shifts[2])
                else:
                    for direction in range(2):
                        gather_copy(slot, direction, hop - 1, hop - 1).wait_recv()
                if hop <= HOPS:
                    for direction in range(2):
                        copy = gather_copy(slot, direction, hop, hop - 1)
                        copy.start()
                        drains.append(copy)
            if step == 1 and first == 0:
                for copy in shifts[:2]:
                    copy.start()
                    drains.append(copy)
                for copy in remote_qd + local_qd:
                    copy.start()
                acc[...] = jnp.zeros_like(acc)

    for t, src in enumerate((q_hbm, do_hbm)):
        local_qd[t].wait()
        mine = src.at[:, pl.ds(pl.multiple_of(g * wide, wide), wide)]
        remote(mine, qd.at[t, other], qd_send.at[t], qd_recv.at[t], partner).wait_recv()
    drains += remote_qd

    def compute(index, carry):
        j = index // 2
        s = index % 2
        window = pl.ds(pl.multiple_of(s * (RING * ROWS) + z * ROWS, ROWS), WIN)
        heads = pl.ds(pl.multiple_of(j * (GROUP_HEADS * HEAD), GROUP_HEADS * HEAD), GROUP_HEADS * HEAD)
        out, gq, gk, gv = attend(
            stack_heads(qd[0, s, :, heads]), stack_heads(qd[1, s, :, heads]),
            kv[j, window, pl.ds(0, HEAD)], kv[j, window, pl.ds(HEAD, HEAD)], start_ref[s],
        )
        for h in range(GROUP_HEADS):
            at = pl.ds(pl.multiple_of(j * (GROUP_HEADS * HEAD) + h * HEAD, HEAD), HEAD)
            og[0, s, :, at] = out[h * ROWS:(h + 1) * ROWS, :]
            og[1, s, :, at] = gq[h * ROWS:(h + 1) * ROWS, :]
        acc[j, window, pl.ds(0, HEAD)] += gk
        acc[j, window, pl.ds(HEAD, HEAD)] += gv
        return carry

    lax.fori_loop(0, 2 * GROUPS, compute, 0)

    own_out = []
    for t, dst in enumerate((o_hbm, gq_hbm)):
        place = dst.at[:, pl.ds(pl.multiple_of(g * wide, wide), wide)]
        copy = remote(og.at[t, other], place, o_send.at[t], o_recv.at[t], partner)
        copy.start()
        drains.append(copy)
        copy = pltpu.make_async_copy(og.at[t, g], place, o_loc.at[t])
        copy.start()
        own_out.append(copy)

    def reduce_copy(slot, direction, hop):
        part = lanes(direction, HOPS + 1 - hop)
        at = (direction, hop - 1, slot)
        return remote(
            ring_out.at[at + (slice(None), slice(None), part)], ring_in.at[at + (slice(None), slice(None), part)],
            rz_send.at[at], rz_recv.at[at], sides[direction],
        )

    def x_copy(slot):
        return remote(x_out.at[slot], x_in.at[slot], rx_send.at[slot], rx_recv.at[slot], behind)

    def own_total(slot):
        total = acc[:, rows(slot, z), :]
        return total + (ring_in[0, HOPS - 1, slot].astype(f32) + ring_in[1, HOPS - 1, slot].astype(f32))

    for step in range(1, HOPS + 4):
        for first, stream in enumerate(reversed(STREAMS)):
            hop = step - first
            if hop < 1 or hop > HOPS + 1:
                continue
            for slot in stream:
                if hop > 1:
                    for direction in range(2):
                        reduce_copy(slot, direction, hop - 1).wait_recv()
                if hop <= HOPS:
                    for direction in range(2):
                        part = lanes(direction, HOPS + 1 - hop)
                        block = rows(slot, block_of(1 - direction, HOPS + 1 - hop))
                        value = acc[:, block, part]
                        if hop == 2:
                            low = ring_in[direction, 0, slot, :, :, pl.ds(direction * HEAD, HEAD)].astype(f32)
                            here = pl.ds(direction * HEAD, HEAD)
                            away = pl.ds((1 - direction) * HEAD, HEAD)
                            ring_out[direction, 1, slot, :, :, here] = (acc[:, block, here] + low).astype(bf16)
                            ring_out[direction, 1, slot, :, :, away] = acc[:, block, away].astype(bf16)
                        else:
                            if hop > 2:
                                value = value + ring_in[direction, hop - 2, slot].astype(f32)
                            ring_out[direction, hop - 1, slot, :, :, part] = value.astype(bf16)
                        copy = reduce_copy(slot, direction, hop)
                        copy.start()
                        drains.append(copy)
                elif slot < 3:
                    total = own_total(slot)
                    if slot == 2:
                        x_copy(0).wait_recv()
                        total = total + x_in[0].astype(f32)
                    x_out[slot] = total.astype(bf16)
                    copy = x_copy(slot)
                    copy.start()
                    drains.append(copy)
                else:
                    total = own_total(slot)
                    x_copy(slot - 2).wait_recv()
                    fin[slot - 3] = (total + x_in[slot - 2].astype(f32)).astype(bf16)

    own_fin = []
    for t, dst in enumerate((gk_hbm, gv_hbm)):
        for j in range(GROUPS):
            place = dst.at[:, cols(j, g)]
            part = pl.ds(t * HEAD, HEAD)
            copy = remote(fin.at[other, j, :, part], place, f_send.at[t, j], f_recv.at[t, j], partner)
            copy.start()
            drains.append(copy)
            copy = pltpu.make_async_copy(fin.at[g, j, :, part], place, f_loc.at[t, j])
            copy.start()
            own_fin.append(copy)

    for copy in own_out + own_fin:
        copy.wait()
    for t, dst in enumerate((o_hbm, gq_hbm)):
        place = dst.at[:, pl.ds(pl.multiple_of(other * wide, wide), wide)]
        remote(og.at[t, g], place, o_send.at[t], o_recv.at[t], partner).wait_recv()
    for t, dst in enumerate((gk_hbm, gv_hbm)):
        for j in range(GROUPS):
            place = dst.at[:, cols(j, other)]
            remote(fin.at[g, j, :, pl.ds(t * HEAD, HEAD)], place, f_send.at[t, j], f_recv.at[t, j], partner).wait_recv()
    for copy in drains:
        copy.wait_send()


def attention(starts, queries, grad_out, keys, values):
    bf16 = jnp.bfloat16
    dma = pltpu.SemaphoreType.DMA
    any_space = pl.BlockSpec(memory_space=pl.ANY)
    wide = GROUPS * GROUP_HEADS * HEAD
    return pl.pallas_call(
        kernel,
        out_shape=(
            jax.ShapeDtypeStruct(queries.shape, bf16),
            jax.ShapeDtypeStruct(queries.shape, bf16),
            jax.ShapeDtypeStruct(keys.shape, bf16),
            jax.ShapeDtypeStruct(keys.shape, bf16),
        ),
        in_specs=[pl.BlockSpec(memory_space=pltpu.VMEM)] + [any_space] * 4,
        out_specs=(any_space,) * 4,
        scratch_shapes=[
            pltpu.VMEM((GROUPS, SLOTS * RING * ROWS, KV), bf16),
            pltpu.VMEM((2, 2, ROWS, wide), bf16),
            pltpu.VMEM((2, 2, ROWS, wide), bf16),
            pltpu.VMEM((GROUPS, SLOTS * RING * ROWS, KV), jnp.float32),
            pltpu.VMEM((2, HOPS, SLOTS, GROUPS, ROWS, KV), bf16),
            pltpu.VMEM((2, HOPS, SLOTS, GROUPS, ROWS, KV), bf16),
            pltpu.VMEM((3, GROUPS, ROWS, KV), bf16),
            pltpu.VMEM((3, GROUPS, ROWS, KV), bf16),
            pltpu.VMEM((2, GROUPS, ROWS, KV), bf16),
            dma((2, GROUPS)), dma((2, GROUPS)), dma((2, GROUPS)),
            dma((2,)), dma((2,)), dma((2,)),
            dma((3,)), dma((3,)),
            dma((SLOTS, 2, HOPS)), dma((SLOTS, 2, HOPS)),
            dma((2, HOPS, SLOTS)), dma((2, HOPS, SLOTS)),
            dma((3,)), dma((3,)),
            dma((2,)), dma((2,)), dma((2,)),
            dma((2, GROUPS)), dma((2, GROUPS)), dma((2, GROUPS)),
        ],
        compiler_params=pltpu.CompilerParams(
            collective_id=0, has_side_effects=True, vmem_limit_bytes=56 * 1024 * 1024
        ),
    )(starts, queries, grad_out, keys, values)


def window_starts(doc_ids, first):
    ids = lax.dynamic_slice_in_dim(doc_ids, first, ROWS)
    begin = jnp.sum((doc_ids[None, :] < ids[:, None]).astype(jnp.int32), axis=1)
    rel = begin - (first - (WIN - ROWS))
    return jnp.tile(rel, 128 // ROWS)[None, :]


def local(queries, keys, values, doc_ids, grad_out):
    first = lax.axis_index("ctx") // 2 * (2 * RING * ROWS) + lax.axis_index("head") * ROWS
    starts = jnp.stack([window_starts(doc_ids, first), window_starts(doc_ids, first + RING * ROWS)])
    return attention(starts, queries, grad_out, keys, values)


def solution(mesh):
    spec = P(("ctx", "head"), None)
    return jax.shard_map(
        local,
        mesh=mesh,
        in_specs=(spec, spec, spec, P(), spec),
        out_specs=(spec, spec, spec, spec),
        check_vma=False,
    )
```

```python
import math

import jax
import jax.numpy as jnp
from jax import lax
from jax.experimental import pallas as pl
from jax.experimental.pallas import tpu as pltpu
from jax.sharding import PartitionSpec as P

HEAD = 128
ROWS = 32
SLOTS = 5
WIN = 800
GROUP_HEADS = 16
GROUPS = 4
KV = 2 * HEAD
RING = 8
HOPS = 4
SCALE = 1.0 / math.sqrt(HEAD)
LOG2E = math.log2(math.e)
NEG = -1e30
MESH = pl.DeviceIdType.MESH
SHIFT = {1: 3, 2: 4, 0: 4}
SPOTS = ((0,), (1, -1), (2, -2), (3, -3), (4,))
ORDER = (4, 3, -3, 2, -2, 1, -1, 0)
CHUNK = 2


def attend(qs, dos, k_win, v_win, start):
    f32, bf16 = jnp.float32, jnp.bfloat16
    q_t = qs.T
    do_t = dos.T.astype(f32)
    kk = lax.broadcasted_iota(jnp.int32, (WIN, 128), 0)
    tt = lax.broadcasted_iota(jnp.int32, (WIN, 128), 1) % ROWS
    allowed = (kk >= start) & (kk <= tt + (WIN - ROWS))
    bias = jnp.where(allowed, 0.0, NEG).astype(f32)
    bias = jnp.concatenate([bias] * (GROUP_HEADS * ROWS // 128), axis=1)
    x = jnp.dot(k_win, q_t, preferred_element_type=f32) * (SCALE * LOG2E) + bias
    top = jnp.max(x, axis=0, keepdims=True)
    p = jnp.exp2(x - top)
    total = jnp.sum(p, axis=0, keepdims=True)
    pb = p.astype(bf16)
    inv = 1.0 / total
    out_t = (jnp.dot(v_win.T, pb, preferred_element_type=f32) * inv).astype(bf16)
    delta = jnp.sum(do_t * out_t.astype(f32), axis=0, keepdims=True) * inv
    do_n = (do_t * inv).astype(bf16)
    gp = jnp.dot(v_win, do_n, preferred_element_type=f32)
    gs = (pb.astype(f32) * (gp - delta)).astype(bf16)
    nt = (((1,), (1,)), ((), ()))
    gv = lax.dot_general(pb, do_n, nt, preferred_element_type=f32)
    gk = jnp.dot(gs, qs, preferred_element_type=f32) * SCALE
    gq_t = (jnp.dot(k_win.T, gs, preferred_element_type=f32) * SCALE).astype(bf16)
    return out_t.T, gq_t.T, gk, gv


def stack_heads(x):
    return jnp.concatenate([x[:, h * HEAD:(h + 1) * HEAD] for h in range(GROUP_HEADS)], axis=0)


def kernel(
    start_ref, q_hbm, do_hbm, k_hbm, v_hbm,
    o_hbm, gq_hbm, gk_hbm, gv_hbm,
    kv, qd, og, acc, ring_out, ring_in, x_out, x_in, fin,
    kv_loc, kv_send, kv_recv, qd_loc, qd_send, qd_recv,
    gx_send, gx_recv, gz_send, gz_recv,
    rz_send, rz_recv, rx_send, rx_recv,
    o_loc, o_send, o_recv, f_loc, f_send, f_recv,
):
    f32, bf16 = jnp.float32, jnp.bfloat16
    c = lax.axis_index("ctx")
    z = lax.axis_index("head")
    n = lax.axis_size("ctx")
    g = lax.rem(c, 2)
    other = 1 - g
    partner = {"ctx": c + 1 - 2 * g, "head": z}
    ahead = {"ctx": lax.rem(c + 2, n), "head": z}
    behind = {"ctx": lax.rem(c + n - 2, n), "head": z}
    ahead2 = {"ctx": lax.rem(c + 4, n), "head": z}
    behind2 = {"ctx": lax.rem(c + n - 4, n), "head": z}
    right = {"ctx": c, "head": lax.rem(z + 1, RING)}
    left = {"ctx": c, "head": lax.rem(z + RING - 1, RING)}
    sides = (right, left)
    half = GROUPS * HEAD
    wide = GROUPS * GROUP_HEADS * HEAD

    barrier = pltpu.get_barrier_semaphore()
    for peer in (partner, ahead, behind, ahead2, behind2, right, left):
        pl.semaphore_signal(barrier, inc=1, device_id=peer, device_id_type=MESH)
    pl.semaphore_wait(barrier, 7)

    def remote(src, dst, send, recv, device):
        return pltpu.make_async_remote_copy(
            src_ref=src, dst_ref=dst, send_sem=send, recv_sem=recv, device_id=device, device_id_type=MESH
        )

    def rows(slot, block):
        return pl.ds(pl.multiple_of(slot * (RING * ROWS) + block * ROWS, ROWS), ROWS)

    def cols(group, which):
        return pl.ds(pl.multiple_of(which * half + group * HEAD, HEAD), HEAD)

    def near(distance):
        return lax.rem(z + distance % RING, RING)

    def members(chunk):
        return pl.ds(chunk * CHUNK, CHUNK)

    drains = []

    def launch(copy):
        copy.start()
        drains.append(copy)

    local_kv, remote_kv = [], []
    for j in range(GROUPS):
        for t, src in enumerate((k_hbm, v_hbm)):
            dst = kv.at[j, rows(3 + g, z), pl.ds(t * HEAD, HEAD)]
            remote_kv.append(remote(src.at[:, cols(j, other)], dst, kv_send.at[t, j], kv_recv.at[t, j], partner))
            local_kv.append(pltpu.make_async_copy(src.at[:, cols(j, g)], dst, kv_loc.at[t, j]))
    for copy in remote_kv:
        launch(copy)
    for copy in local_kv:
        copy.start()
    local_qd, remote_qd = [], []
    for t, src in enumerate((q_hbm, do_hbm)):
        mine = src.at[:, pl.ds(pl.multiple_of(g * wide, wide), wide)]
        theirs = src.at[:, pl.ds(pl.multiple_of(other * wide, wide), wide)]
        remote_qd.append(remote(theirs, qd.at[t, g], qd_send.at[t], qd_recv.at[t], partner))
        local_qd.append(pltpu.make_async_copy(mine, qd.at[t, g], qd_loc.at[t]))
    for copy in local_kv:
        copy.wait()

    def await_own(chunk):
        for t, src in enumerate((k_hbm, v_hbm)):
            for j in range(chunk * CHUNK, (chunk + 1) * CHUNK):
                dst = kv.at[j, rows(3 + other, z), pl.ds(t * HEAD, HEAD)]
                remote(src.at[:, cols(j, g)], dst, kv_send.at[t, j], kv_recv.at[t, j], partner).wait_recv()

    def lanes(direction, hop):
        if hop < HOPS:
            return pl.ds(0, KV)
        return pl.ds(direction * HEAD, HEAD)

    def gather_copy(chunk, slot, direction, hop, distance):
        block = kv.at[members(chunk), rows(slot, near(distance)), lanes(direction, hop)]
        at = (chunk, slot, direction, hop - 1)
        return remote(block, block, gz_send.at[at], gz_recv.at[at], sides[direction])

    def gather_wait(chunk, slot, hop):
        for direction, sign in enumerate((-1, 1)):
            gather_copy(chunk, slot, direction, hop, sign * hop).wait_recv()

    def gather_hop(chunk, slot, hop):
        for direction, sign in enumerate((-1, 1)):
            launch(gather_copy(chunk, slot, direction, hop, sign * (hop - 1)))

    def shift_copy(chunk, target, distance):
        source = SHIFT[target]
        at = (chunk, target, distance % RING)
        block = near(distance)
        return remote(
            kv.at[members(chunk), rows(source, block), :], kv.at[members(chunk), rows(target, block), :],
            gx_send.at[at], gx_recv.at[at], ahead if target else ahead2,
        )

    def gather_far(chunk, step):
        if step == 0:
            launch(shift_copy(chunk, 0, 0))
        elif step == 1:
            shift_copy(chunk, 0, 0).wait_recv()
        else:
            gather_wait(chunk, 0, step - 1)
        if 1 <= step <= HOPS:
            gather_hop(chunk, 0, step)

    def gather_x_first(chunk):
        for step in range(HOPS + 2):
            for slot in (4, 3):
                if 1 <= step <= HOPS:
                    gather_wait(chunk, slot, step)
                if step < HOPS:
                    gather_hop(chunk, slot, step + 1)
                if step == 0:
                    launch(shift_copy(chunk, slot - 2, 0))
            for slot in (2, 1):
                if step == 1:
                    shift_copy(chunk, slot, 0).wait_recv()
                elif step > 1:
                    gather_wait(chunk, slot, step - 1)
                if 1 <= step <= HOPS:
                    gather_hop(chunk, slot, step)
            gather_far(chunk, step)
            yield

    def gather_z_first(chunk):
        for step in range(HOPS + 2):
            if step <= HOPS:
                for slot in (4, 3):
                    if step > 0:
                        gather_wait(chunk, slot, step)
                    if step < HOPS:
                        gather_hop(chunk, slot, step + 1)
                    for distance in SPOTS[step]:
                        launch(shift_copy(chunk, slot - 2, distance))
            gather_far(chunk, step)
            if step > HOPS:
                for spot in SPOTS:
                    for distance in spot:
                        for slot in (2, 1):
                            shift_copy(chunk, slot, distance).wait_recv()
            yield

    def attend_rows(j, s):
        window = pl.ds(pl.multiple_of(s * (RING * ROWS) + z * ROWS, ROWS), WIN)
        heads = pl.ds(pl.multiple_of(j * (GROUP_HEADS * HEAD), GROUP_HEADS * HEAD), GROUP_HEADS * HEAD)
        out, gq, gk, gv = attend(
            stack_heads(qd[0, s, :, heads]), stack_heads(qd[1, s, :, heads]),
            kv[j, window, pl.ds(0, HEAD)], kv[j, window, pl.ds(HEAD, HEAD)], start_ref[s],
        )
        for h in range(GROUP_HEADS):
            at = pl.ds(pl.multiple_of(j * (GROUP_HEADS * HEAD) + h * HEAD, HEAD), HEAD)
            og[0, s, :, at] = out[h * ROWS:(h + 1) * ROWS, :]
            og[1, s, :, at] = gq[h * ROWS:(h + 1) * ROWS, :]
        acc[j, window, pl.ds(0, HEAD)] += gk
        acc[j, window, pl.ds(HEAD, HEAD)] += gv

    def reduce_copy(j, slot, direction, hop):
        part = lanes(direction, HOPS + 1 - hop)
        at = (j, direction, hop - 1, slot)
        view = at + (slice(None), part)
        return remote(ring_out.at[view], ring_in.at[view], rz_send.at[at], rz_recv.at[at], sides[direction])

    def reduce_wait(j, slot, hop):
        for direction in range(2):
            reduce_copy(j, slot, direction, hop).wait_recv()

    def reduce_hop(j, slot, hop):
        for direction, sign in enumerate((1, -1)):
            block = rows(slot, near(sign * (HOPS + 1 - hop)))
            out = (j, direction, hop - 1, slot, slice(None))
            came = (j, direction, hop - 2, slot, slice(None))
            if hop == 2:
                here = pl.ds(direction * HEAD, HEAD)
                away = pl.ds((1 - direction) * HEAD, HEAD)
                ring_out[out + (here,)] = (acc[j, block, here] + ring_in[came + (here,)].astype(f32)).astype(bf16)
                ring_out[out + (away,)] = acc[j, block, away].astype(bf16)
            else:
                part = lanes(direction, HOPS + 1 - hop)
                value = acc[j, block, part]
                if hop > 2:
                    value = value + ring_in[came + (part,)].astype(f32)
                ring_out[out + (part,)] = value.astype(bf16)
            launch(reduce_copy(j, slot, direction, hop))

    def ring_total(j, slot):
        total = acc[j, rows(slot, z), :]
        return total + (ring_in[j, 0, HOPS - 1, slot].astype(f32) + ring_in[j, 1, HOPS - 1, slot].astype(f32))

    def x_copy(j, slot, distance):
        at = (j, slot, distance % RING)
        device = behind if slot else behind2
        return remote(x_out.at[at], x_in.at[at], rx_send.at[at], rx_recv.at[at], device)

    def send_total(j, slot):
        x_out[j, slot, 0] = ring_total(j, slot).astype(bf16)
        launch(x_copy(j, slot, 0))

    def ring_step(j, slot, step):
        if step > 0:
            reduce_wait(j, slot, step)
        if step < HOPS:
            reduce_hop(j, slot, step + 1)

    def reduce_z_first(j):
        for step in range(HOPS + 2):
            if step <= HOPS:
                for slot in (0, 2, 1):
                    ring_step(j, slot, step)
                    if step == HOPS:
                        send_total(j, slot)
                for slot in (4, 3):
                    ring_step(j, slot, step)
            else:
                for slot in (4, 3):
                    total = ring_total(j, slot)
                    x_copy(j, slot - 2, 0).wait_recv()
                    total = total + x_in[j, slot - 2, 0].astype(f32)
                    if slot == 4:
                        x_copy(j, 0, 0).wait_recv()
                        total = total + x_in[j, 0, 0].astype(f32)
                    fin[slot - 3, j] = total.astype(bf16)
            yield

    def reduce_x_first(j):
        for step in range(HOPS + 2):
            if step > 0:
                for slot in (4, 3):
                    for distance in SPOTS[HOPS + 1 - step]:
                        x_copy(j, slot - 2, distance).wait_recv()
                        place = rows(slot, near(distance))
                        acc[j, place, :] = acc[j, place, :] + x_in[j, slot - 2, distance % RING].astype(f32)
                    ring_step(j, slot, step - 1)
            if step <= HOPS:
                ring_step(j, 0, step)
                if step == HOPS:
                    send_total(j, 0)
            if step == 0:
                for distance in ORDER:
                    for slot in (2, 1):
                        x_out[j, slot, distance % RING] = acc[j, rows(slot, near(distance)), :].astype(bf16)
                        launch(x_copy(j, slot, distance))
            if step > HOPS:
                fin[0, j] = ring_total(j, 3).astype(bf16)
                total = ring_total(j, 4)
                x_copy(j, 0, 0).wait_recv()
                fin[1, j] = (total + x_in[j, 0, 0].astype(f32)).astype(bf16)
            yield

    own_fin = []

    def finish(j):
        for t, dst in enumerate((gk_hbm, gv_hbm)):
            place = dst.at[:, cols(j, g)]
            part = pl.ds(t * HEAD, HEAD)
            launch(remote(fin.at[other, j, :, part], place, f_send.at[t, j], f_recv.at[t, j], partner))
            copy = pltpu.make_async_copy(fin.at[g, j, :, part], place, f_loc.at[t, j])
            copy.start()
            own_fin.append(copy)

    z_first, x_first = gather_z_first(0), gather_x_first(1)
    await_own(0)
    next(z_first)
    await_own(1)
    next(x_first)
    for copy in remote_qd:
        launch(copy)
    for copy in local_qd:
        copy.start()
    acc[...] = jnp.zeros_like(acc)
    next(z_first)
    for step in range(HOPS):
        next(z_first)
        if step < HOPS - 1:
            next(x_first)

    for t, src in enumerate((q_hbm, do_hbm)):
        local_qd[t].wait()
        mine = src.at[:, pl.ds(pl.multiple_of(g * wide, wide), wide)]
        remote(mine, qd.at[t, other], qd_send.at[t], qd_recv.at[t], partner).wait_recv()

    backs = []
    for j in range(GROUPS):
        if j == 0:
            for s in range(2):
                attend_rows(j, s)
                next(x_first)
        else:
            lax.fori_loop(0, 2, lambda s, carry, j=j: (attend_rows(j, s), carry)[1], 0)
        backs.insert(0, reduce_z_first(j) if j < CHUNK else reduce_x_first(j))
        for back in backs:
            next(back)

    own_out = []
    for t, dst in enumerate((o_hbm, gq_hbm)):
        place = dst.at[:, pl.ds(pl.multiple_of(g * wide, wide), wide)]
        launch(remote(og.at[t, other], place, o_send.at[t], o_recv.at[t], partner))
        copy = pltpu.make_async_copy(og.at[t, g], place, o_loc.at[t])
        copy.start()
        own_out.append(copy)

    for step in range(1, HOPS + 2):
        for index, back in enumerate(backs):
            if step + index < HOPS + 2:
                next(back)
                if step + index == HOPS + 1:
                    finish(GROUPS - 1 - index)

    for copy in own_out + own_fin:
        copy.wait()
    for t, dst in enumerate((o_hbm, gq_hbm)):
        place = dst.at[:, pl.ds(pl.multiple_of(other * wide, wide), wide)]
        remote(og.at[t, g], place, o_send.at[t], o_recv.at[t], partner).wait_recv()
    for t, dst in enumerate((gk_hbm, gv_hbm)):
        for j in range(GROUPS):
            place = dst.at[:, cols(j, other)]
            remote(fin.at[g, j, :, pl.ds(t * HEAD, HEAD)], place, f_send.at[t, j], f_recv.at[t, j], partner).wait_recv()
    for copy in drains:
        copy.wait_send()


def attention(starts, queries, grad_out, keys, values):
    bf16 = jnp.bfloat16
    dma = pltpu.SemaphoreType.DMA
    any_space = pl.BlockSpec(memory_space=pl.ANY)
    wide = GROUPS * GROUP_HEADS * HEAD
    chunks = GROUPS // CHUNK
    return pl.pallas_call(
        kernel,
        out_shape=(
            jax.ShapeDtypeStruct(queries.shape, bf16),
            jax.ShapeDtypeStruct(queries.shape, bf16),
            jax.ShapeDtypeStruct(keys.shape, bf16),
            jax.ShapeDtypeStruct(keys.shape, bf16),
        ),
        in_specs=[pl.BlockSpec(memory_space=pltpu.VMEM)] + [any_space] * 4,
        out_specs=(any_space,) * 4,
        scratch_shapes=[
            pltpu.VMEM((GROUPS, SLOTS * RING * ROWS, KV), bf16),
            pltpu.VMEM((2, 2, ROWS, wide), bf16),
            pltpu.VMEM((2, 2, ROWS, wide), bf16),
            pltpu.VMEM((GROUPS, SLOTS * RING * ROWS, KV), jnp.float32),
            pltpu.VMEM((GROUPS, 2, HOPS, SLOTS, ROWS, KV), bf16),
            pltpu.VMEM((GROUPS, 2, HOPS, SLOTS, ROWS, KV), bf16),
            pltpu.VMEM((GROUPS, 3, RING, ROWS, KV), bf16),
            pltpu.VMEM((GROUPS, 3, RING, ROWS, KV), bf16),
            pltpu.VMEM((2, GROUPS, ROWS, KV), bf16),
            dma((2, GROUPS)), dma((2, GROUPS)), dma((2, GROUPS)),
            dma((2,)), dma((2,)), dma((2,)),
            dma((chunks, 3, RING)), dma((chunks, 3, RING)),
            dma((chunks, SLOTS, 2, HOPS)), dma((chunks, SLOTS, 2, HOPS)),
            dma((GROUPS, 2, HOPS, SLOTS)), dma((GROUPS, 2, HOPS, SLOTS)),
            dma((GROUPS, 3, RING)), dma((GROUPS, 3, RING)),
            dma((2,)), dma((2,)), dma((2,)),
            dma((2, GROUPS)), dma((2, GROUPS)), dma((2, GROUPS)),
        ],
        compiler_params=pltpu.CompilerParams(
            collective_id=0, has_side_effects=True, vmem_limit_bytes=58 * 1024 * 1024
        ),
    )(starts, queries, grad_out, keys, values)


def window_starts(doc_ids, first):
    ids = lax.dynamic_slice_in_dim(doc_ids, first, ROWS)
    begin = jnp.sum((doc_ids[None, :] < ids[:, None]).astype(jnp.int32), axis=1)
    rel = begin - (first - (WIN - ROWS))
    return jnp.tile(rel, 128 // ROWS)[None, :]


def local(queries, keys, values, doc_ids, grad_out):
    first = lax.axis_index("ctx") // 2 * (2 * RING * ROWS) + lax.axis_index("head") * ROWS
    starts = jnp.stack([window_starts(doc_ids, first), window_starts(doc_ids, first + RING * ROWS)])
    return attention(starts, queries, grad_out, keys, values)


def solution(mesh):
    spec = P(("ctx", "head"), None)
    return jax.shard_map(
        local,
        mesh=mesh,
        in_specs=(spec, spec, spec, P(), spec),
        out_specs=(spec, spec, spec, spec),
        check_vma=False,
    )
```
